32 devices in a mesh: dp: 2 (over x), expert: 16 (over z, y, core).
Axes of the slice: x: 2, y: 2, z: 4, core: 2. Of those that a mesh axis runs over, the one named last changes fastest.
Arguments:
- expert_out: bfloat16 [2, 128, 16, 2, 7168], P('dp', 'expert'), may hold values from -6 to 6
- expert_ids: int32 [256, 8], P(('dp', 'expert')), may hold values from 0 to 127, all different within a row; in each aligned block of 8 rows (0 to 7, 8 to 15, ...) at most 2 rows name the same one
- gate_weight: float32 [256, 8], P(('dp', 'expert')), may hold values from 0.05 to 1
Outputs:
- combined: bfloat16 [256, 7168], P(('dp', 'expert'))
- expert_counts: int32 [128], P('expert')
- expert_rms: float32 [128], P('expert')
The draws below stay inside these ranges and needn't reach their ends.
Inputs may be any that keep to these rules, and one draw needn't show every extreme that they name: `expert_ids`: in each aligned block of 8 tokens no expert is named by more than 2 rows, and a token names 8 different experts; every expert is named by some token.
All inputs are finite; a program needn't handle non-finite values.
Results may differ from the reference program's by a relative error of at most 0.008.
Values may be sent and summed in bfloat16 or wider, within the bound.
No kernel may reach another device: no remote copies, remote signals or barrier semaphores. Data moves between devices by JAX's collectives and lax.ppermute only.
A program may use at most 64 MiB of HBM per device.

```python
import math
import jax
import jax.numpy as jnp
import numpy as np
from jax import lax

D = 7168
EXPERTS = 128
TOP = 8
TOK_DEV = 8
CAP = 2
TOKENS = 256
N_DP = 2
N_EXPERT = 16


def steps_of(stream_key, dims, pieces, low, high):
    gain, own = 1.0, jax.random.fold_in(stream_key, 6)
    for axis_at, blocks in pieces:
        steps = jnp.exp(jax.random.uniform(jax.random.fold_in(own, axis_at), (blocks,), jnp.float32, low / len(pieces), high / len(pieces)))
        gain = gain * jnp.repeat(steps, dims[axis_at] // blocks).reshape([-1 if axis == axis_at else 1 for axis in range(len(dims))])
    return gain


def shared_out(stream_key, own, number, rows, amount, top, bound, slope):
    sequence = jax.random.permutation(stream_key, amount)
    crowded, common = load_shares(amount, rows * top, bound, slope, True), load_shares(amount, rows * top, bound, slope, False)
    places = jnp.arange(amount)

    def named(tallies, offset_by):
        used = int((tallies > 0).sum())
        fixed = max(1, used // 4)
        moved = fixed + (places - fixed + offset_by * (used - fixed)) % max(1, amount - fixed)
        return jnp.zeros((amount,), jnp.int32).at[sequence[jnp.where(places < fixed, places, moved)]].set(jnp.asarray(tallies, jnp.int32))

    tallies = jnp.where(number % 4 == 0, named(crowded, number // 4), named(common, number - number // 4 - 1))
    mixed = jax.random.permutation(jax.random.fold_in(own, 3), amount)
    giver, sink = mixed[0:amount // 2 * 2:2], mixed[1:amount // 2 * 2:2]
    margin = jnp.minimum(tallies[giver] - 1, bound - tallies[sink]) // 2
    margin = jnp.where((giver == sequence[0]) | (sink == sequence[0]) | (tallies[sink] == 0), 0, jnp.maximum(margin, 0))
    moved = jax.random.randint(jax.random.fold_in(own, 4), (amount // 2,), 0, 1 << 20) % (margin + 1)
    tallies = tallies.at[giver].add(-moved).at[sink].add(moved)
    members = jnp.searchsorted(jnp.cumsum(tallies), jnp.arange(rows * top), side="right").astype(jnp.int32)
    listing = members.reshape(top, rows).T
    listing = listing[jax.random.permutation(jax.random.fold_in(own, 1), rows)]
    offset_by = jax.random.randint(jax.random.fold_in(own, 2), (rows, 1), 0, top)
    return jnp.take_along_axis(listing, (jnp.arange(top)[None, :] + offset_by) % top, axis=1)


def load_shares(amount, total, most, slope, full):
    weights = [(1 << 20) // math.isqrt(grade ** slope) + 1 for grade in range(1, amount + 1)]
    largest = most if full else min(most, max(-(-total // amount), total * weights[0] // sum(weights)))
    least = 1 if total - largest >= amount - 1 else 0
    given, spare = [largest] + [least] * (amount - 1), total - largest - least * (amount - 1)
    while spare > 0:
        movable = [i for i in range(1, amount) if given[i] < largest] or [i for i in range(1, amount) if given[i] < most]
        whole, budget = sum([weights[i] for i in movable]), spare
        for i in movable:
            more = min(most - given[i], max(1, budget * weights[i] // whole), spare)
            given[i] = given[i] + more
            spare = spare - more
    return np.array(given)


def scatter_about(own_key, shape, spread, reach, pieces=(), kind=jnp.bfloat16):
    factor_of = steps_of(own_key, shape, pieces, -0.22, 0.18) if pieces else 1.0
    values = jax.random.normal(own_key, shape, jnp.float32) * spread * factor_of
    return jnp.minimum(jnp.maximum(values, -reach), reach).astype(kind)


def setup_inputs(seed: int = 0) -> dict:
    splits = jax.random.split(jax.random.key(seed), 4)
    expert_out = scatter_about(splits[0], (N_DP, EXPERTS, N_EXPERT, CAP, D), 1.0, 6.0, ((0, 2), (1, 16)))
    expert_ids_keys = jax.random.split(jax.random.fold_in(splits[1], 1), TOKENS // TOK_DEV)
    expert_ids_turns = jax.random.permutation(jax.random.fold_in(splits[1], 3), TOKENS // TOK_DEV)
    expert_ids = jax.vmap(lambda own, number: shared_out(jax.random.fold_in(splits[1], 2), own, number, TOK_DEV, EXPERTS, TOP, CAP, 2))(expert_ids_keys, expert_ids_turns).reshape((TOKENS, TOP))
    gate_weight = jnp.clip(0.05 + 0.95 * jax.random.uniform(splits[2], (TOKENS, TOP), jnp.float32) ** steps_of(splits[2], (TOKENS, TOP), ((0, 32),), -0.2, 0.2), 0.05, 1.0)
    return {"expert_out": expert_out, "expert_ids": expert_ids, "gate_weight": gate_weight}


epsilon = 1e-06

def slot_index_of(block_ids):
    flat = block_ids.reshape(-1).astype(jnp.int32)
    total_rows = flat.shape[0]
    one_hot = (flat[:, None] == jnp.arange(EXPERTS, dtype=jnp.int32)[None, :]).astype(jnp.float32)
    earlier = (jnp.arange(total_rows, dtype=jnp.int32)[:, None] > jnp.arange(total_rows, dtype=jnp.int32)[None, :]).astype(jnp.float32)
    before = jnp.dot(earlier, one_hot, precision=lax.Precision.HIGHEST)
    position = lax.optimization_barrier(jnp.sum(before * one_hot, axis=1)).astype(jnp.int32)
    return flat * CAP + position

def holder_combine(picked, ids, gates, per_holder):
    holder = ids // per_holder
    same = (holder[:, :, None] == holder[:, None, :]).astype(jnp.float32)
    weights = same * gates[:, None, :].astype(jnp.float32)
    partial_value = jnp.einsum('tkj,tjd->tkd', weights, picked.astype(jnp.float32), precision=lax.Precision.HIGHEST)
    partial_value = partial_value.astype(jnp.bfloat16).astype(jnp.float32)
    lower = (jnp.arange(TOP, dtype=jnp.int32)[:, None] > jnp.arange(TOP, dtype=jnp.int32)[None, :]).astype(jnp.float32)
    repeats = lax.optimization_barrier(jnp.sum(same * lower[None, :, :], axis=2))
    leading = (repeats < 0.5).astype(jnp.float32)
    return lax.optimization_barrier(jnp.sum(leading[:, :, None] * partial_value, axis=1)).astype(jnp.bfloat16)

def reference(expert_out, expert_ids, gate_weight):
    blocks = N_DP * N_EXPERT
    per_holder = EXPERTS // N_EXPERT
    id_blocks = expert_ids.reshape(blocks, TOK_DEV, TOP)
    gate_blocks = gate_weight.reshape(blocks, TOK_DEV, TOP)

    def one_block(block_id):
        group = block_id // N_EXPERT
        source = block_id % N_EXPERT
        slab = lax.dynamic_index_in_dim(expert_out, group, 0, keepdims=False)
        slab = lax.dynamic_index_in_dim(slab, source, 1, keepdims=False)
        received = slab.reshape(EXPERTS * CAP, D)
        block_ids = lax.dynamic_index_in_dim(id_blocks, block_id, 0, keepdims=False)
        gates = lax.dynamic_index_in_dim(gate_blocks, block_id, 0, keepdims=False)
        slot_index = slot_index_of(block_ids)
        picked = jnp.take(received, slot_index, axis=0).reshape(TOK_DEV, TOP, D)
        mixed_block = holder_combine(picked, block_ids, gates, per_holder)
        occupied = lax.optimization_barrier(jnp.sum((slot_index[:, None] == jnp.arange(EXPERTS * CAP, dtype=jnp.int32)[None, :]).astype(jnp.float32), axis=0))
        squares = lax.optimization_barrier(jnp.sum(jnp.square(received.astype(jnp.float32)), axis=1))
        sum_squares = lax.optimization_barrier(jnp.sum((occupied * squares).reshape(EXPERTS, CAP), axis=1))
        count_part = lax.optimization_barrier(jnp.sum(occupied.reshape(EXPERTS, CAP), axis=1))
        return (mixed_block, sum_squares, count_part)
    mixed_blocks, sums, counts = lax.map(one_block, jnp.arange(blocks, dtype=jnp.int32))
    combined = mixed_blocks.reshape(TOKENS, D)
    total_counts = lax.optimization_barrier(jnp.sum(counts, axis=0))
    total_squares = lax.optimization_barrier(jnp.sum(sums, axis=0))
    expert_rms = jnp.sqrt(total_squares / (total_counts * D) + epsilon)
    return (combined, total_counts.astype(jnp.int32), expert_rms)
```

```python
import functools

import jax
import jax.numpy as jnp
from jax import lax
from jax.experimental import pallas as pl
from jax.experimental.pallas import tpu as pltpu
from jax.sharding import PartitionSpec as P

LANES = 128
GROUP = 8

epsilon = 1e-06


def weights_of(block, lane_expert, lane_slot, top):
    tokens = block.shape[0]
    shape = (tokens, lane_expert.shape[1])
    named = jnp.zeros(shape, jnp.float32)
    gate = jnp.zeros(shape, jnp.float32)
    for k in range(top):
        same = jnp.broadcast_to(block[:, k : k + 1], shape) == lane_expert
        named = named + jnp.where(same, 1.0, 0.0)
        gate = gate + jnp.where(same, jnp.broadcast_to(block[:, top + k : top + k + 1], shape), 0.0)
    row = lax.broadcasted_iota(jnp.int32, shape, 0)
    earlier = named
    shift = 1
    while shift < tokens:
        earlier = earlier + jnp.where(row >= shift, pltpu.roll(earlier, shift, 0), 0.0)
        shift *= 2
    earlier = earlier - named
    return jnp.where(earlier == lane_slot, gate, 0.0)


def combine_kernel(me_ref, gates_ref, own_hbm, other_hbm, out_ref, buffer, sems, *, sources, first, last, top, cap):
    me = me_ref[0]
    experts, tokens = own_hbm.shape[0], gates_ref.shape[1]
    rows = GROUP * cap
    span = pl.ds(first * rows, (last - first) * rows)

    def copies(i):
        source = ((me >> 1) ^ sources(i)) * 2 + (me & 1)
        return source, [
            pltpu.make_async_copy(ref.at[:, source, span, :], buffer.at[i, h], sems.at[i, h])
            for h, ref in enumerate((own_hbm, other_hbm))
        ]

    @pl.loop(0, out_ref.shape[0])
    def _(i):
        for copy in copies(i)[1]:
            copy.start()

    depth = 2 * experts * rows
    lane = lax.broadcasted_iota(jnp.int32, (tokens, depth), 1)
    local = (lane // rows) % experts
    holder = jnp.where(lane < experts * rows, me, me ^ 1)
    lane_expert = (holder * experts + local).astype(jnp.float32)
    lane_slot = (lane % cap).astype(jnp.float32)
    wide = lax.broadcasted_iota(jnp.int32, (GROUP, tokens, depth), 2)
    same_tile = (wide // cap) % GROUP == lax.broadcasted_iota(jnp.int32, wide.shape, 0)

    @pl.loop(0, out_ref.shape[0])
    def _(i):
        source, waits = copies(i)
        weights = weights_of(gates_ref[source], lane_expert, lane_slot, top)
        weights = jnp.where(same_tile, jnp.broadcast_to(weights[None], wide.shape), 0.0)
        weights = weights.reshape(GROUP * tokens, depth)
        high = weights.astype(jnp.bfloat16)
        low = (weights - high.astype(jnp.float32)).astype(jnp.bfloat16)
        both = jnp.concatenate([high, low], axis=0)
        for copy in waits:
            copy.wait()
        for b in range(last - first):
            part = buffer[i, :, :, b * rows : (b + 1) * rows, :].reshape(depth, LANES)
            total = jnp.dot(both, part, preferred_element_type=jnp.float32)
            total = total[: GROUP * tokens] + total[GROUP * tokens :]
            out_ref[i, b * GROUP * tokens : (b + 1) * GROUP * tokens, :] = total.astype(out_ref.dtype)


def combine(me, gates, own, other, sources, count, first, last, top, cap):
    experts = own.shape[0]
    tokens = gates.shape[1]
    rows = (last - first) * GROUP
    kernel = functools.partial(
        combine_kernel, sources=sources, first=first, last=last, top=top, cap=cap
    )
    return pl.pallas_call(
        kernel,
        out_shape=jax.ShapeDtypeStruct((count, rows * tokens, LANES), jnp.bfloat16),
        in_specs=[
            pl.BlockSpec(memory_space=pltpu.SMEM),
            pl.BlockSpec(memory_space=pltpu.VMEM),
            pl.BlockSpec(memory_space=pl.ANY),
            pl.BlockSpec(memory_space=pl.ANY),
        ],
        out_specs=pl.BlockSpec(memory_space=pltpu.VMEM),
        scratch_shapes=[
            pltpu.VMEM((count, 2, experts, rows * cap, LANES), jnp.bfloat16),
            pltpu.SemaphoreType.DMA((count, 2)),
        ],
        name="combine",
    )(me, gates, own, other)


def statistics_kernel(me_ref, gates_ref, own_ref, sums_ref, counts_ref, *, top, cap):
    step = pl.program_id(0)
    experts, height = own_ref.shape[0], own_ref.shape[2]
    tokens = gates_ref.shape[1]
    rows = GROUP * cap
    depth = experts * rows

    @pl.when(step == 0)
    def _():
        sums_ref[...] = jnp.zeros_like(sums_ref)
        counts_ref[...] = jnp.zeros_like(counts_ref)

    lane = lax.broadcasted_iota(jnp.int32, (tokens, depth), 1)
    lane_expert = (me_ref[0] * experts + lane // rows).astype(jnp.float32)
    block = gates_ref[0]
    named = jnp.zeros((tokens, depth), jnp.float32)
    for k in range(top):
        named = named + jnp.where(jnp.broadcast_to(block[:, k : k + 1], named.shape) == lane_expert, 1.0, 0.0)
    times = jnp.sum(named, axis=0, keepdims=True)
    shape = (experts, depth)
    lane = lax.broadcasted_iota(jnp.int32, shape, 1)
    mine = lane // rows == lax.broadcasted_iota(jnp.int32, shape, 0)
    used = jnp.where(
        mine & (jnp.broadcast_to(times, shape) > (lane % cap).astype(jnp.float32)), 1.0, 0.0
    )
    counts_ref[...] = counts_ref[...] + used
    used = used.astype(jnp.bfloat16)
    total = sums_ref[...]
    for b in range(height // rows):
        part = own_ref[:, 0, b * rows : (b + 1) * rows, :].reshape(depth, LANES).astype(jnp.float32)
        part = part * part
        high = part.astype(jnp.bfloat16)
        low = (part - high.astype(jnp.float32)).astype(jnp.bfloat16)
        total = total + jnp.dot(used, high, preferred_element_type=jnp.float32)
        total = total + jnp.dot(used, low, preferred_element_type=jnp.float32)
    sums_ref[...] = total


def statistics(me, gates, own, top, cap):
    experts, holders, height, _ = own.shape
    depth = experts * GROUP * cap
    return pl.pallas_call(
        functools.partial(statistics_kernel, top=top, cap=cap),
        grid_spec=pltpu.PrefetchScalarGridSpec(
            num_scalar_prefetch=1,
            grid=(holders,),
            in_specs=[
                pl.BlockSpec((1,) + gates.shape[1:], lambda s, me: (s, 0, 0)),
                pl.BlockSpec((experts, 1, height, LANES), lambda s, me: (0, s, 0, 0)),
            ],
            out_specs=[
                pl.BlockSpec((experts, LANES), lambda s, me: (0, 0)),
                pl.BlockSpec((experts, depth), lambda s, me: (0, 0)),
            ],
        ),
        out_shape=[
            jax.ShapeDtypeStruct((experts, LANES), jnp.float32),
            jax.ShapeDtypeStruct((experts, depth), jnp.float32),
        ],
        name="statistics",
    )(me, gates, own)


def exchange(x, axis, size, bit):
    return lax.ppermute(x, axis, [(i, i ^ bit) for i in range(size)])


def body(dp, holders, expert_out, expert_ids, gate_weight):
    _, experts, _, cap, width = expert_out.shape
    tokens, top = expert_ids.shape
    tiles = width // LANES
    me = lax.axis_index("expert").astype(jnp.int32).reshape(1)
    own = expert_out.reshape(experts, holders, cap, tiles, LANES)
    own = own.transpose(0, 1, 3, 2, 4).reshape(experts, holders, tiles * cap, LANES)
    other = exchange(own, "expert", holders, 1)
    packed = jnp.concatenate([expert_ids.astype(jnp.float32), gate_weight], axis=1)
    gates = jnp.broadcast_to(packed[None], (holders,) + packed.shape)
    gates = lax.all_to_all(gates, "expert", split_axis=0, concat_axis=0, tiled=True)

    chips = holders // 2
    low = 1 << ((chips.bit_length() - 1) // 2)
    high = chips // low
    groups = tiles // GROUP
    cut = (groups + 1) // 2
    totals = []
    for first, last in ((0, cut), (cut, groups)):
        def part(digit):
            return combine(
                me, gates, own, other, lambda i: i * low + digit, high, first, last, top, cap
            )
        total = [part(d) for d in range(1, low)]
        moved = [exchange(t, "expert", holders, 2 * (d + 1)) for d, t in enumerate(total)]
        kept = part(0).astype(jnp.float32)
        for m in moved:
            kept = kept + m.astype(jnp.float32)
        kept = kept.astype(jnp.bfloat16)
        result = kept[0].astype(jnp.float32)
        for d in range(1, high):
            result = result + exchange(kept[d], "expert", holders, 2 * low * d).astype(jnp.float32)
        totals.append(result.astype(jnp.bfloat16))
    combined = jnp.concatenate(totals, axis=0).reshape(tiles, tokens, LANES)
    combined = combined.transpose(1, 0, 2).reshape(tokens, width)

    sums, counts = statistics(me, gates, own, top, cap)
    sums = jnp.sum(sums, axis=1)
    counts = jnp.sum(counts, axis=1) / GROUP
    both = jnp.stack([sums, counts])
    bit = 1
    while bit < dp:
        both = both + exchange(both, "dp", dp, bit)
        bit *= 2
    expert_rms = jnp.sqrt(both[0] / (both[1] * width) + epsilon)
    return combined, both[1].astype(jnp.int32), expert_rms


def solution(mesh):
    return jax.shard_map(
        functools.partial(body, mesh.shape["dp"], mesh.shape["expert"]),
        mesh=mesh,
        in_specs=(
            P("dp", "expert", None, None, None),
            P(("dp", "expert"), None),
            P(("dp", "expert"), None),
        ),
        out_specs=(P(("dp", "expert"), None), P("expert"), P("expert")),
        check_vma=False,
    )
```

```python
import functools

import jax
import jax.numpy as jnp
from jax import lax
from jax.experimental import pallas as pl
from jax.experimental.pallas import tpu as pltpu
from jax.sharding import PartitionSpec as P


LANES = 128
GROUP = 8

epsilon = 1e-06

VMEM = pl.BlockSpec(memory_space=pltpu.VMEM)
SMEM = pl.BlockSpec(memory_space=pltpu.SMEM)
HBM = pl.BlockSpec(memory_space=pltpu.HBM)


def iota(shape, axis):
    return lax.broadcasted_iota(jnp.int32, shape, axis)


def params():
    return pltpu.CompilerParams(vmem_limit_bytes=16 << 20)


def near(x):
    return pltpu.with_memory_space_constraint(x, pltpu.VMEM)


def far(x):
    return pltpu.with_memory_space_constraint(x, pltpu.HBM)


def split(x):
    high = x.astype(jnp.bfloat16)
    return high, (x - high.astype(jnp.float32)).astype(jnp.bfloat16)


def weights_kernel(ids_hbm, gates_hbm, out_ref, ids_ref, gates_ref, sems):
    loads = [
        pltpu.make_async_copy(ids_hbm, ids_ref, sems.at[0]),
        pltpu.make_async_copy(gates_hbm, gates_ref, sems.at[1]),
    ]
    for copy in loads:
        copy.start()
    for copy in loads:
        copy.wait()
    _, tokens, experts = out_ref.shape
    ids, gates = ids_ref[...], gates_ref[...]
    shape = (tokens, experts)
    lane, row = iota(shape, 1), iota(shape, 0)
    gate = jnp.zeros(shape, jnp.float32)
    named = jnp.zeros(shape, jnp.float32)
    for k in range(ids.shape[1]):
        same = jnp.broadcast_to(ids[:, k : k + 1], shape) == lane
        named = jnp.where(same, 1.0, named)
        gate = jnp.where(same, jnp.broadcast_to(gates[:, k : k + 1], shape), gate)
    upto, shift = named, 1
    while shift < tokens:
        upto = upto + jnp.where(row >= shift, pltpu.roll(upto, shift, 0), 0.0)
        shift *= 2
    signed = jnp.where(upto - named > 0.5, -gate, gate)
    out_ref[...] = jnp.broadcast_to(signed[None], out_ref.shape)


def weights(ids, gates, holders, experts):
    return pl.pallas_call(
        weights_kernel,
        out_shape=pltpu.VMEM((holders, ids.shape[0], experts), jnp.float32),
        in_specs=[HBM, HBM],
        out_specs=VMEM,
        scratch_shapes=[
            pltpu.VMEM(ids.shape, ids.dtype),
            pltpu.VMEM(gates.shape, gates.dtype),
            pltpu.SemaphoreType.DMA((2,)),
        ],
        compiler_params=params(),
        name="weights",
    )(far(ids), far(gates))


def prepare_kernel(me_ref, own_hbm, other_hbm, squares_ref, send_ref, own_ref, sems, send_sems, *, sources):
    me = me_ref[0]
    experts, holders, height, _ = own_hbm.shape
    loads = [pltpu.make_async_copy(own_hbm.at[e], own_ref.at[e], sems.at[e]) for e in range(experts)]
    for copy in loads:
        copy.start()
    sends = []
    for i, q in enumerate(sources):
        source = ((me >> 1) ^ q) * 2 + (me & 1)
        for h, ref in enumerate((own_hbm, other_hbm)):
            sends.append(pltpu.make_async_copy(ref.at[:, source], send_ref.at[i, h], send_sems.at[i, h]))
    for copy in sends:
        copy.start()
    ones = jnp.ones((8, LANES), jnp.bfloat16)
    for e in range(experts):
        loads[e].wait()
        parts = []
        for s in range(holders):
            total = jnp.zeros((8, LANES), jnp.float32)
            for r in range(0, height, 16):
                part = own_ref[e, s, r : r + 16, :].astype(jnp.float32)
                total = total + part[:8] * part[:8] + part[8:] * part[8:]
            parts.append(total)
        total = jnp.concatenate(parts, axis=0)
        sums = jnp.zeros((8, holders * 8), jnp.float32)
        for term in split(total):
            sums = sums + lax.dot_general(
                ones, term, (((1,), (1,)), ((), ())), preferred_element_type=jnp.float32
            )
        squares_ref[e] = sums
    for copy in sends:
        copy.wait()


def prepare(me, own, other, sources):
    experts, holders, height, _ = own.shape
    return pl.pallas_call(
        functools.partial(prepare_kernel, sources=sources),
        in_specs=[SMEM, HBM, HBM],
        out_specs=[VMEM, VMEM],
        out_shape=[
            pltpu.VMEM((experts, 8, holders * 8), jnp.float32),
            pltpu.VMEM((len(sources), 2, experts, height, LANES), own.dtype),
        ],
        scratch_shapes=[
            pltpu.VMEM(own.shape, own.dtype),
            pltpu.SemaphoreType.DMA((experts,)),
            pltpu.SemaphoreType.DMA((len(sources), 2)),
        ],
        compiler_params=params(),
        name="prepare",
    )(me, far(own), far(other))


def statistics_kernel(me_ref, signed_ref, squares_ref, out_ref, *, cap):
    holders, _, every = signed_ref.shape
    experts = squares_ref.shape[0]
    wide = squares_ref.shape[2]
    signed = signed_ref[...]
    mine = jnp.where(
        iota((experts, every), 1) == me_ref[0] * experts + iota((experts, every), 0), 1.0, 0.0
    ).astype(jnp.bfloat16)
    spread = iota((holders, wide), 1) // 8 == iota((holders, wide), 0)
    slot = iota((experts, wide), 1) % cap
    row = iota((experts, wide), 0)
    total = jnp.zeros((experts, wide), jnp.float32)
    for c, used in enumerate((signed > 0.0, signed < 0.0)):
        used = jnp.max(jnp.where(used, 1.0, 0.0), axis=1).astype(jnp.bfloat16)
        used = lax.dot_general(
            mine, used, (((1,), (1,)), ((), ())), preferred_element_type=jnp.float32
        )
        used = jnp.dot(
            used.astype(jnp.bfloat16),
            jnp.where(spread, 1.0, 0.0).astype(jnp.bfloat16),
            preferred_element_type=jnp.float32,
        )
        total = jnp.where(slot == c, used, total)
    square = jnp.zeros((experts, wide), jnp.float32)
    for e in range(experts):
        square = jnp.where(row == e, jnp.broadcast_to(squares_ref[e, 0:1, :], square.shape), square)
    sums = jnp.sum(total * square, axis=1, keepdims=True)
    counts = jnp.sum(total, axis=1, keepdims=True) * (cap / 8)
    out_ref[...] = jnp.where(iota(out_ref.shape, 1) < LANES // 2, sums, counts)


def statistics(me, signed, square, cap):
    return pl.pallas_call(
        functools.partial(statistics_kernel, cap=cap),
        out_shape=pltpu.VMEM((square.shape[0], LANES), jnp.float32),
        in_specs=[SMEM, VMEM, VMEM],
        out_specs=VMEM,
        compiler_params=params(),
        name="statistics",
    )(me, near(signed), near(square))


def lefts(me, signed_ref, source, experts, cap):
    tokens, every = signed_ref.shape[1:]
    rows = GROUP * cap
    depth = 2 * experts * rows
    lane = iota((every, depth), 1)
    holder = jnp.where(lane < experts * rows, me, me ^ 1)
    chosen = iota((every, depth), 0) == holder * experts + (lane // rows) % experts
    chosen = jnp.where(chosen, 1.0, 0.0).astype(jnp.bfloat16)
    signed = jnp.concatenate([signed_ref[s] for s in source], axis=0)
    high, low = split(signed)
    high = jnp.dot(high, chosen, preferred_element_type=jnp.float32)
    low = jnp.dot(low, chosen, preferred_element_type=jnp.float32)
    second = high < 0.0
    keep = second == (iota(high.shape, 1) % cap == 1)
    sign = jnp.where(second, -1.0, 1.0)
    high = jnp.where(keep, high * sign, 0.0)
    low = jnp.where(keep, low * sign, 0.0)
    tile = (iota((tokens, depth), 1) // cap) % GROUP
    for i in range(len(source)):
        span = slice(i * tokens, (i + 1) * tokens)
        left = [jnp.where(tile == j, term[span], 0.0) for term in (high, low) for j in range(GROUP)]
        yield jnp.concatenate(left, axis=0).astype(jnp.bfloat16)


def weighted(left, part):
    total = jnp.dot(left, part.reshape(-1, LANES), preferred_element_type=jnp.float32)
    half = left.shape[0] // 2
    return total[:half] + total[half:]


def send_kernel(me_ref, signed_ref, rows_ref, out_ref, *, sources, first, last, cap):
    me = me_ref[0]
    rows, high = GROUP * cap, GROUP * signed_ref.shape[1]
    source = [((me >> 1) ^ q) * 2 + (me & 1) for q in sources]
    for i, left in enumerate(lefts(me, signed_ref, source, rows_ref.shape[2], cap)):
        for b in range(last - first):
            total = weighted(left, rows_ref[i, :, :, (first + b) * rows : (first + b + 1) * rows, :])
            out_ref[i, b * high : (b + 1) * high, :] = total.astype(out_ref.dtype)


def send(me, signed, rows, sources, first, last, cap):
    height = (last - first) * GROUP * signed.shape[1]
    return pl.pallas_call(
        functools.partial(send_kernel, sources=sources, first=first, last=last, cap=cap),
        out_shape=pltpu.VMEM((len(sources), height, LANES), rows.dtype),
        in_specs=[SMEM, VMEM, VMEM],
        out_specs=VMEM,
        compiler_params=params(),
        name="send",
    )(me, near(signed), near(rows))


def keep_kernel(me_ref, signed_ref, own_hbm, other_hbm, out_ref, buffer, sems, *, sources, cap):
    me = me_ref[0]
    rows, high = GROUP * cap, GROUP * signed_ref.shape[1]
    source = [((me >> 1) ^ q) * 2 + (me & 1) for q in sources]
    copies = [
        [
            pltpu.make_async_copy(ref.at[:, s], buffer.at[i, h], sems.at[i, h])
            for h, ref in enumerate((own_hbm, other_hbm))
        ]
        for i, s in enumerate(source)
    ]
    for pair in copies:
        for copy in pair:
            copy.start()
    for i, left in enumerate(lefts(me, signed_ref, source, own_hbm.shape[0], cap)):
        for copy in copies[i]:
            copy.wait()
        for b in range(own_hbm.shape[2] // rows):
            total = weighted(left, buffer[i, :, :, b * rows : (b + 1) * rows, :])
            out_ref[i, b * high : (b + 1) * high, :] = total


def keep(me, signed, own, other, sources, cap):
    experts, _, height, _ = own.shape
    return pl.pallas_call(
        functools.partial(keep_kernel, sources=sources, cap=cap),
        out_shape=pltpu.VMEM((len(sources), height // cap * signed.shape[1], LANES), jnp.float32),
        in_specs=[SMEM, VMEM, HBM, HBM],
        out_specs=VMEM,
        scratch_shapes=[
            pltpu.VMEM((len(sources), 2, experts, height, LANES), own.dtype),
            pltpu.SemaphoreType.DMA((len(sources), 2)),
        ],
        compiler_params=params(),
        name="keep",
    )(me, near(signed), far(own), far(other))


def exchange(x, axis, size, bit):
    return lax.ppermute(x, axis, [(i, i ^ bit) for i in range(size)])


def body(dp, holders, expert_out, expert_ids, gate_weight):
    _, experts, _, cap, width = expert_out.shape
    tokens = expert_ids.shape[0]
    tiles = width // LANES
    me = lax.axis_index("expert").astype(jnp.int32).reshape(1)
    own = expert_out.reshape(experts, holders, cap, tiles, LANES)
    own = own.transpose(0, 1, 3, 2, 4).reshape(experts, holders, tiles * cap, LANES)
    other = exchange(own, "expert", holders, 1)
    signed = weights(expert_ids, gate_weight, holders, experts * holders)
    signed = lax.all_to_all(signed, "expert", split_axis=0, concat_axis=0, tiled=True)
    chips = holders // 2
    low = 1 << ((chips.bit_length() - 1) // 2)
    high = chips // low
    groups = tiles // GROUP
    cut = (groups + 1) // 2
    sources = [[i * low + digit for i in range(high)] for digit in range(low)]
    square, rows = prepare(me, own, other, [q for some in sources[1:] for q in some])
    chunks = ((0, cut), (cut, groups))
    moved = []
    for first, last in chunks:
        part = send(me, signed, rows, [q for some in sources[1:] for q in some], first, last, cap)
        part = part.reshape(low - 1, high, -1, LANES)
        moved.append([exchange(part[d - 1], "expert", holders, 2 * d) for d in range(1, low)])
    kept = keep(me, signed, own, other, sources[0], cap)
    totals = []
    for (first, last), some in zip(chunks, moved):
        total = kept[:, first * GROUP * tokens : last * GROUP * tokens]
        for m in some:
            total = total + m.astype(jnp.float32)
        result = total[0]
        for d in range(1, high):
            m = exchange(total[d].astype(jnp.bfloat16), "expert", holders, 2 * low * d)
            result = result + m.astype(jnp.float32)
        totals.append(result.astype(jnp.bfloat16))
    combined = jnp.concatenate(totals, axis=0).reshape(tiles, tokens, LANES)
    combined = combined.transpose(1, 0, 2).reshape(tokens, width)

    both = statistics(me, signed, square, cap)
    bit = 1
    while bit < dp:
        other = exchange(both, "dp", dp, bit)
        both = both + other
        bit *= 2
    sums, counts = both[:, 0], both[:, LANES - 1]
    expert_rms = jnp.sqrt(sums / (counts * width) + epsilon)
    counts = counts.astype(jnp.int32)
    return combined, counts, expert_rms


def solution(mesh):
    def step(*args):
        return body(mesh.shape["dp"], mesh.shape["expert"], *args)

    step = jax.shard_map(
        step,
        mesh=mesh,
        in_specs=(
            P("dp", "expert", None, None, None),
            P(("dp", "expert"), None),
            P(("dp", "expert"), None),
        ),
        out_specs=(P(("dp", "expert"), None), P("expert"), P("expert")),
        check_vma=False,
    )
    return step
```

```python
import functools

import jax
import jax.numpy as jnp
from jax import lax
from jax.experimental import pallas as pl
from jax.experimental.pallas import tpu as pltpu
from jax.sharding import PartitionSpec as P


LANES = 128
GROUP = 8

epsilon = 1e-06

VMEM = pl.BlockSpec(memory_space=pltpu.VMEM)
SMEM = pl.BlockSpec(memory_space=pltpu.SMEM)
HBM = pl.BlockSpec(memory_space=pltpu.HBM)


def iota(shape, axis):
    return lax.broadcasted_iota(jnp.int32, shape, axis)


def params():
    return pltpu.CompilerParams(vmem_limit_bytes=16 << 20)


def near(x):
    return pltpu.with_memory_space_constraint(x, pltpu.VMEM)


def far(x):
    return pltpu.with_memory_space_constraint(x, pltpu.HBM)


def split(x):
    high = x.astype(jnp.bfloat16)
    return high, (x - high.astype(jnp.float32)).astype(jnp.bfloat16)


def weights_kernel(ids_hbm, gates_hbm, out_ref, ids_ref, gates_ref, sems):
    loads = [
        pltpu.make_async_copy(ids_hbm, ids_ref, sems.at[0]),
        pltpu.make_async_copy(gates_hbm, gates_ref, sems.at[1]),
    ]
    for copy in loads:
        copy.start()
    for copy in loads:
        copy.wait()
    tokens = out_ref.shape[0]
    ids, gates = ids_ref[...], gates_ref[...]
    shape = out_ref.shape
    lane, row = iota(shape, 1), iota(shape, 0)
    gate = jnp.zeros(shape, jnp.float32)
    named = jnp.zeros(shape, jnp.float32)
    for k in range(ids.shape[1]):
        same = jnp.broadcast_to(ids[:, k : k + 1], shape) == lane
        named = jnp.where(same, 1.0, named)
        gate = jnp.where(same, jnp.broadcast_to(gates[:, k : k + 1], shape), gate)
    upto, shift = named, 1
    while shift < tokens:
        upto = upto + jnp.where(row >= shift, pltpu.roll(upto, shift, 0), 0.0)
        shift *= 2
    out_ref[...] = jnp.where(upto - named > 0.5, -gate, gate)


def weights(ids, gates, experts):
    return pl.pallas_call(
        weights_kernel,
        out_shape=pltpu.VMEM((ids.shape[0], experts), jnp.float32),
        in_specs=[HBM, HBM],
        out_specs=VMEM,
        scratch_shapes=[
            pltpu.VMEM(ids.shape, ids.dtype),
            pltpu.VMEM(gates.shape, gates.dtype),
            pltpu.SemaphoreType.DMA((2,)),
        ],
        compiler_params=params(),
        name="weights",
    )(far(ids), far(gates))


def load_kernel(own_hbm, own_ref, sem):
    copy = pltpu.make_async_copy(own_hbm, own_ref, sem)
    copy.start()
    copy.wait()


def load(own):
    return pl.pallas_call(
        load_kernel,
        out_shape=pltpu.VMEM(own.shape, own.dtype),
        in_specs=[HBM],
        out_specs=VMEM,
        scratch_shapes=[pltpu.SemaphoreType.DMA],
        compiler_params=params(),
        name="load",
    )(far(own))


def squares_kernel(own_ref, out_ref):
    experts, holders, height, _ = own_ref.shape
    ones = jnp.ones((8, LANES), jnp.bfloat16)
    for e in range(experts):
        parts = []
        for s in range(holders):
            total = jnp.zeros((8, LANES), jnp.float32)
            for r in range(0, height, 16):
                part = own_ref[e, s, r : r + 16, :].astype(jnp.float32)
                total = total + part[:8] * part[:8] + part[8:] * part[8:]
            parts.append(total)
        total = jnp.concatenate(parts, axis=0)
        sums = jnp.zeros((8, holders * 8), jnp.float32)
        for term in split(total):
            sums = sums + lax.dot_general(
                ones, term, (((1,), (1,)), ((), ())), preferred_element_type=jnp.float32
            )
        out_ref[e] = sums


def squares(own):
    experts, holders, _, _ = own.shape
    return pl.pallas_call(
        squares_kernel,
        out_shape=pltpu.VMEM((experts, 8, holders * 8), jnp.float32),
        in_specs=[VMEM],
        out_specs=VMEM,
        compiler_params=params(),
        name="squares",
    )(near(own))


def statistics_kernel(mine_ref, theirs_ref, squares_ref, out_ref, *, cap):
    me = lax.axis_index("expert")
    chips, _, every = mine_ref.shape
    experts, _, wide = squares_ref.shape
    mine = jnp.where(
        iota((experts, every), 1) == me * experts + iota((experts, every), 0), 1.0, 0.0
    ).astype(jnp.bfloat16)
    slot = iota((experts, wide), 1) % cap
    row = iota((experts, wide), 0)
    total = jnp.zeros((experts, wide), jnp.float32)
    for core, ref in enumerate((mine_ref, theirs_ref)):
        signed = ref[...]
        source = (iota((chips, wide), 0) * 2 + core) ^ me
        spread = jnp.where(iota((chips, wide), 1) // 8 == source, 1.0, 0.0).astype(jnp.bfloat16)
        for c, used in enumerate((signed > 0.0, signed < 0.0)):
            used = jnp.max(jnp.where(used, 1.0, 0.0), axis=1).astype(jnp.bfloat16)
            used = lax.dot_general(
                mine, used, (((1,), (1,)), ((), ())), preferred_element_type=jnp.float32
            )
            used = jnp.dot(used.astype(jnp.bfloat16), spread, preferred_element_type=jnp.float32)
            total = total + jnp.where(slot == c, used, 0.0)
    square = jnp.zeros((experts, wide), jnp.float32)
    for e in range(experts):
        square = jnp.where(row == e, jnp.broadcast_to(squares_ref[e, 0:1, :], square.shape), square)
    sums = jnp.sum(total * square, axis=1, keepdims=True)
    counts = jnp.sum(total, axis=1, keepdims=True) * (cap / 8)
    out_ref[...] = jnp.where(iota(out_ref.shape, 1) < LANES // 2, sums, counts)


def statistics(mine, theirs, square, cap):
    return pl.pallas_call(
        functools.partial(statistics_kernel, cap=cap),
        out_shape=pltpu.VMEM((square.shape[0], LANES), jnp.float32),
        in_specs=[VMEM, VMEM, VMEM],
        out_specs=VMEM,
        compiler_params=params(),
        name="statistics",
    )(near(mine), near(theirs), near(square))


def combine_kernel(signed_ref, own_ref, other_ref, out_ref, *, sources, first, last, cap):
    me = lax.axis_index("expert")
    experts = own_ref.shape[0]
    tokens, every = signed_ref.shape[1:]
    rows = GROUP * cap
    depth = 2 * experts * rows
    lane = iota((every, depth), 1)
    holder = jnp.where(lane < experts * rows, me, me ^ 1)
    chosen = iota((every, depth), 0) == holder * experts + (lane // rows) % experts
    chosen = jnp.where(chosen, 1.0, 0.0).astype(jnp.bfloat16)
    signed = signed_ref[...].reshape(-1, every)
    high, low = split(signed)
    high = jnp.dot(high, chosen, preferred_element_type=jnp.float32)
    low = jnp.dot(low, chosen, preferred_element_type=jnp.float32)
    second = high < 0.0
    kept = second == (iota(high.shape, 1) % cap == 1)
    sign = jnp.where(second, -1.0, 1.0)
    high = jnp.where(kept, high * sign, 0.0)
    low = jnp.where(kept, low * sign, 0.0)
    tile = (iota((tokens, depth), 1) // cap) % GROUP
    half = GROUP * tokens
    for i, q in enumerate(sources):
        source = me ^ (2 * q)
        span = slice(i * tokens, (i + 1) * tokens)
        left = [jnp.where(tile == j, term[span], 0.0) for term in (high, low) for j in range(GROUP)]
        left = jnp.concatenate(left, axis=0).astype(jnp.bfloat16)
        for b in range(first, last):
            part = slice(b * rows, (b + 1) * rows)
            part = jnp.concatenate([own_ref[:, source, part, :], other_ref[:, source, part, :]], axis=0)
            total = jnp.dot(left, part.reshape(depth, LANES), preferred_element_type=jnp.float32)
            total = total[:half] + total[half:]
            out_ref[i, (b - first) * half : (b - first + 1) * half, :] = total.astype(out_ref.dtype)


def combine(signed, own, other, sources, first, last, cap, dtype):
    rows = (last - first) * GROUP
    return pl.pallas_call(
        functools.partial(combine_kernel, sources=sources, first=first, last=last, cap=cap),
        out_shape=pltpu.VMEM((len(sources), rows * signed.shape[1], LANES), dtype),
        in_specs=[VMEM, VMEM, VMEM],
        out_specs=VMEM,
        compiler_params=params(),
    )(near(signed), near(own), near(other))


def exchange(x, axis, size, bit):
    return lax.ppermute(x, axis, [(i, i ^ bit) for i in range(size)])


def body(dp, holders, expert_out, expert_ids, gate_weight):
    _, experts, _, cap, width = expert_out.shape
    tokens = expert_ids.shape[0]
    tiles = width // LANES
    groups = tiles // GROUP
    chips = holders // 2
    low = 1 << ((chips.bit_length() - 1) // 2)
    high = chips // low

    def swap(x, bit):
        return exchange(x, "expert", holders, bit)

    own = expert_out.reshape(experts, holders, cap, tiles, LANES)
    own = own.transpose(0, 1, 3, 2, 4).reshape(experts, holders, tiles * cap, LANES)
    other = swap(own, 1)
    tile = weights(expert_ids, gate_weight, experts * holders)
    signed = jnp.stack([tile] + [swap(tile, 2 * d) for d in range(1, low)])
    own = load(own)
    signed = [signed]
    for h in range(1, high):
        signed.append(swap(signed[0], 2 * low * h))

    def sums(pairs, first, last, dtype):
        tiles = jnp.concatenate([signed[h][d : d + 1] for h, d in pairs])
        sources = [h * low + d for h, d in pairs]
        return combine(tiles, own, other, sources, first, last, cap, dtype)

    part = sums([(1, d) for d in range(low)], 0, groups, jnp.bfloat16)
    near_sums = swap(part, 2 * low).astype(jnp.float32)
    cut = (groups + 1) // 2
    chunks = {"c": (0, cut), "d": (cut, groups)}
    distant = list(range(2, high))
    arrived = {}
    for key, (first, last) in chunks.items():
        part = sums([(h, d) for d in range(1, low) for h in distant], first, last, jnp.bfloat16)
        part = part.reshape(low - 1, len(distant), -1, LANES)
        arrived[key] = [swap(part[d - 1], 2 * d) for d in range(1, low)]
    kept = sums([(0, d) for d in range(low)] + [(h, 0) for h in distant], 0, groups, jnp.float32)
    combined = kept[0] + near_sums[0]
    for d in range(1, low):
        moved = swap((kept[d] + near_sums[d]).astype(jnp.bfloat16), 2 * d)
        combined = combined + moved.astype(jnp.float32)

    def second(key, i):
        first, last = chunks[key]
        out = kept[low + i, first * GROUP * tokens : last * GROUP * tokens]
        for m in arrived[key]:
            out = out + m[i].astype(jnp.float32)
        return swap(out.astype(jnp.bfloat16), 2 * low * distant[i]).astype(jnp.float32)

    moved = {key: [second(key, i) for i in range(len(distant))] for key in chunks}
    combined = combined + jnp.concatenate([sum(some[1:], some[0]) for some in moved.values()])
    combined = combined.astype(jnp.bfloat16).reshape(tiles, tokens, LANES)
    combined = combined.transpose(1, 0, 2).reshape(tokens, width)

    signed = jnp.concatenate(signed)
    theirs = swap(signed, 1)
    square = squares(own)
    both = statistics(signed, theirs, square, cap)
    bit = 1
    while bit < dp:
        moved = exchange(both, "dp", dp, bit)
        both = both + moved
        bit *= 2
    squared, counts = both[:, 0], both[:, LANES - 1]
    expert_rms = jnp.sqrt(squared / (counts * width) + epsilon)
    counts = counts.astype(jnp.int32)
    return combined, counts, expert_rms


def solution(mesh):
    def step(*args):
        return body(mesh.shape["dp"], mesh.shape["expert"], *args)

    step = jax.shard_map(
        step,
        mesh=mesh,
        in_specs=(
            P("dp", "expert", None, None, None),
            P(("dp", "expert"), None),
            P(("dp", "expert"), None),
        ),
        out_specs=(P(("dp", "expert"), None), P("expert"), P("expert")),
        check_vma=False,
    )
    return step
```

```python
import functools

import jax
import jax.numpy as jnp
from jax import lax
from jax.experimental import pallas as pl
from jax.experimental.pallas import tpu as pltpu
from jax.sharding import PartitionSpec as P


LANES = 128
GROUP = 8

epsilon = 1e-06

VMEM = pl.BlockSpec(memory_space=pltpu.VMEM)
SMEM = pl.BlockSpec(memory_space=pltpu.SMEM)
HBM = pl.BlockSpec(memory_space=pltpu.HBM)


def iota(shape, axis):
    return lax.broadcasted_iota(jnp.int32, shape, axis)


def params():
    return pltpu.CompilerParams(vmem_limit_bytes=16 << 20)


def near(x):
    return pltpu.with_memory_space_constraint(x, pltpu.VMEM)


def far(x):
    return pltpu.with_memory_space_constraint(x, pltpu.HBM)


def split(x):
    high = x.astype(jnp.bfloat16)
    return high, (x - high.astype(jnp.float32)).astype(jnp.bfloat16)


def weights_kernel(ids_hbm, gates_hbm, out_ref, ids_ref, gates_ref, sems):
    loads = [
        pltpu.make_async_copy(ids_hbm, ids_ref, sems.at[0]),
        pltpu.make_async_copy(gates_hbm, gates_ref, sems.at[1]),
    ]
    for copy in loads:
        copy.start()
    for copy in loads:
        copy.wait()
    tokens = out_ref.shape[0]
    ids, gates = ids_ref[...], gates_ref[...]
    shape = out_ref.shape
    lane, row = iota(shape, 1), iota(shape, 0)
    gate = jnp.zeros(shape, jnp.float32)
    named = jnp.zeros(shape, jnp.float32)
    for k in range(ids.shape[1]):
        same = jnp.broadcast_to(ids[:, k : k + 1], shape) == lane
        named = jnp.where(same, 1.0, named)
        gate = jnp.where(same, jnp.broadcast_to(gates[:, k : k + 1], shape), gate)
    upto, shift = named, 1
    while shift < tokens:
        upto = upto + jnp.where(row >= shift, pltpu.roll(upto, shift, 0), 0.0)
        shift *= 2
    out_ref[...] = jnp.where(upto - named > 0.5, -gate, gate)


def weights(ids, gates, experts):
    return pl.pallas_call(
        weights_kernel,
        out_shape=pltpu.VMEM((ids.shape[0], experts), jnp.float32),
        in_specs=[HBM, HBM],
        out_specs=VMEM,
        scratch_shapes=[
            pltpu.VMEM(ids.shape, ids.dtype),
            pltpu.VMEM(gates.shape, gates.dtype),
            pltpu.SemaphoreType.DMA((2,)),
        ],
        compiler_params=params(),
        name="weights",
    )(far(ids), far(gates))


def load_kernel(own_hbm, own_ref, sem):
    copy = pltpu.make_async_copy(own_hbm, own_ref, sem)
    copy.start()
    copy.wait()


def load(own):
    return pl.pallas_call(
        load_kernel,
        out_shape=pltpu.VMEM(own.shape, own.dtype),
        in_specs=[HBM],
        out_specs=VMEM,
        scratch_shapes=[pltpu.SemaphoreType.DMA],
        compiler_params=params(),
        name="load",
    )(far(own))


def squares_kernel(own_ref, out_ref):
    experts, holders, height, _ = own_ref.shape
    ones = jnp.ones((8, LANES), jnp.bfloat16)
    for e in range(experts):
        parts = []
        for s in range(holders):
            total = jnp.zeros((8, LANES), jnp.float32)
            for r in range(0, height, 16):
                part = own_ref[e, s, r : r + 16, :].astype(jnp.float32)
                total = total + part[:8] * part[:8] + part[8:] * part[8:]
            parts.append(total)
        total = jnp.concatenate(parts, axis=0)
        sums = jnp.zeros((8, holders * 8), jnp.float32)
        for term in split(total):
            sums = sums + lax.dot_general(
                ones, term, (((1,), (1,)), ((), ())), preferred_element_type=jnp.float32
            )
        out_ref[e] = sums


def squares(own):
    experts, holders, _, _ = own.shape
    return pl.pallas_call(
        squares_kernel,
        out_shape=pltpu.VMEM((experts, 8, holders * 8), jnp.float32),
        in_specs=[VMEM],
        out_specs=VMEM,
        compiler_params=params(),
        name="squares",
    )(near(own))


def statistics_kernel(mine_ref, theirs_ref, squares_ref, out_ref, *, cap):
    me = lax.axis_index("expert")
    chips, _, every = mine_ref.shape
    experts, _, wide = squares_ref.shape
    mine = jnp.where(
        iota((experts, every), 1) == me * experts + iota((experts, every), 0), 1.0, 0.0
    ).astype(jnp.bfloat16)
    slot = iota((experts, wide), 1) % cap
    row = iota((experts, wide), 0)
    total = jnp.zeros((experts, wide), jnp.float32)
    for core, ref in enumerate((mine_ref, theirs_ref)):
        signed = ref[...]
        source = (iota((chips, wide), 0) * 2 + core) ^ me
        spread = jnp.where(iota((chips, wide), 1) // 8 == source, 1.0, 0.0).astype(jnp.bfloat16)
        for c, used in enumerate((signed > 0.0, signed < 0.0)):
            used = jnp.max(jnp.where(used, 1.0, 0.0), axis=1).astype(jnp.bfloat16)
            used = lax.dot_general(
                mine, used, (((1,), (1,)), ((), ())), preferred_element_type=jnp.float32
            )
            used = jnp.dot(used.astype(jnp.bfloat16), spread, preferred_element_type=jnp.float32)
            total = total + jnp.where(slot == c, used, 0.0)
    square = jnp.zeros((experts, wide), jnp.float32)
    for e in range(experts):
        square = jnp.where(row == e, jnp.broadcast_to(squares_ref[e, 0:1, :], square.shape), square)
    ones = jnp.ones((8, wide), jnp.float32)
    sums, counts = [
        lax.dot_general(
            ones, x, (((1,), (1,)), ((), ())),
            precision=lax.Precision.HIGHEST, preferred_element_type=jnp.float32,
        )
        for x in (total * square, total * (cap / 8))
    ]
    out_ref[...] = jnp.where(iota(out_ref.shape, 0) == 0, sums, counts)


def statistics(mine, theirs, square, cap):
    return pl.pallas_call(
        functools.partial(statistics_kernel, cap=cap),
        out_shape=pltpu.VMEM((8, square.shape[0]), jnp.float32),
        in_specs=[VMEM, VMEM, VMEM],
        out_specs=VMEM,
        compiler_params=params(),
        name="statistics",
    )(near(mine), near(theirs), near(square))


def combine_kernel(signed_ref, own_ref, other_ref, out_ref, *, sources, first, last, cap):
    me = lax.axis_index("expert")
    experts = own_ref.shape[0]
    tokens, every = signed_ref.shape[1:]
    rows = GROUP * cap
    depth = 2 * experts * rows
    lane = iota((every, depth), 1)
    holder = jnp.where(lane < experts * rows, me, me ^ 1)
    chosen = iota((every, depth), 0) == holder * experts + (lane // rows) % experts
    chosen = jnp.where(chosen, 1.0, 0.0).astype(jnp.bfloat16)
    signed = signed_ref[...].reshape(-1, every)
    high, low = split(signed)
    high = jnp.dot(high, chosen, preferred_element_type=jnp.float32)
    low = jnp.dot(low, chosen, preferred_element_type=jnp.float32)
    second = high < 0.0
    kept = second == (iota(high.shape, 1) % cap == 1)
    sign = jnp.where(second, -1.0, 1.0)
    high = jnp.where(kept, high * sign, 0.0)
    low = jnp.where(kept, low * sign, 0.0)
    tile = (iota((tokens, depth), 1) // cap) % GROUP
    half = GROUP * tokens
    for i, q in enumerate(sources):
        source = me ^ (2 * q)
        span = slice(i * tokens, (i + 1) * tokens)
        left = [jnp.where(tile == j, term[span], 0.0) for term in (high, low) for j in range(GROUP)]
        left = jnp.concatenate(left, axis=0).astype(jnp.bfloat16)
        for b in range(first, last):
            part = slice(b * rows, (b + 1) * rows)
            part = jnp.concatenate([own_ref[:, source, part, :], other_ref[:, source, part, :]], axis=0)
            total = jnp.dot(left, part.reshape(depth, LANES), preferred_element_type=jnp.float32)
            total = total[:half] + total[half:]
            out_ref[i, (b - first) * half : (b - first + 1) * half, :] = total.astype(out_ref.dtype)


def combine(signed, own, other, sources, first, last, cap, dtype):
    rows = (last - first) * GROUP
    return pl.pallas_call(
        functools.partial(combine_kernel, sources=sources, first=first, last=last, cap=cap),
        out_shape=pltpu.VMEM((len(sources), rows * signed.shape[1], LANES), dtype),
        in_specs=[VMEM, VMEM, VMEM],
        out_specs=VMEM,
        compiler_params=params(),
    )(near(signed), near(own), near(other))


def exchange(x, axis, size, bit):
    return lax.ppermute(x, axis, [(i, i ^ bit) for i in range(size)])


def body(dp, holders, expert_out, expert_ids, gate_weight):
    _, experts, _, cap, width = expert_out.shape
    tokens = expert_ids.shape[0]
    tiles = width // LANES
    groups = tiles // GROUP
    chips = holders // 2
    low = 1 << ((chips.bit_length() - 1) // 2)
    high = chips // low

    def swap(x, bit):
        return exchange(x, "expert", holders, bit)

    own = expert_out.reshape(experts, holders, cap, tiles, LANES)
    own = own.transpose(0, 1, 3, 2, 4).reshape(experts, holders, tiles * cap, LANES)
    other = swap(own, 1)
    tile = weights(expert_ids, gate_weight, experts * holders)
    signed = jnp.stack([tile] + [swap(tile, 2 * d) for d in range(1, low)])
    own = load(own)
    signed = [signed]
    for h in range(1, high):
        signed.append(swap(signed[0], 2 * low * h))

    def sums(pairs, first, last, dtype):
        tiles = jnp.concatenate([signed[h][d : d + 1] for h, d in pairs])
        sources = [h * low + d for h, d in pairs]
        return combine(tiles, own, other, sources, first, last, cap, dtype)

    part = sums([(1, d) for d in range(low)], 0, groups, jnp.bfloat16)
    near_sums = swap(part, 2 * low).astype(jnp.float32)
    cut = groups // 2
    chunks = {"c": (0, cut), "d": (cut, groups)}
    distant = list(range(2, high))
    arrived = {}
    for key, (first, last) in chunks.items():
        part = sums([(h, d) for d in range(1, low) for h in distant], first, last, jnp.bfloat16)
        part = part.reshape(low - 1, len(distant), -1, LANES)
        arrived[key] = [swap(part[d - 1], 2 * d) for d in range(1, low)]
    kept = sums([(0, d) for d in range(low)] + [(h, 0) for h in distant], 0, groups, jnp.float32)
    combined = kept[0] + near_sums[0]
    for d in range(1, low):
        moved = swap((kept[d] + near_sums[d]).astype(jnp.bfloat16), 2 * d)
        combined = combined + moved.astype(jnp.float32)

    def second(key, i):
        first, last = chunks[key]
        out = kept[low + i, first * GROUP * tokens : last * GROUP * tokens]
        for m in arrived[key]:
            out = out + m[i].astype(jnp.float32)
        return swap(out.astype(jnp.bfloat16), 2 * low * distant[i]).astype(jnp.float32)

    moved = {key: [second(key, i) for i in range(len(distant))] for key in chunks}
    combined = combined + jnp.concatenate([sum(some[1:], some[0]) for some in moved.values()])
    combined = combined.astype(jnp.bfloat16).reshape(tiles, tokens, LANES)
    combined = combined.transpose(1, 0, 2).reshape(tokens, width)

    signed = jnp.concatenate(signed)
    theirs = swap(signed, 1)
    square = squares(own)
    both = statistics(signed, theirs, square, cap)
    bit = 1
    while bit < dp:
        moved = exchange(both, "dp", dp, bit)
        both = both + moved
        bit *= 2
    squared, counts = both[0], both[1]
    expert_rms = jnp.sqrt(squared / (counts * width) + epsilon)
    counts = counts.astype(jnp.int32)
    return combined, counts, expert_rms


def solution(mesh):
    def step(*args):
        return body(mesh.shape["dp"], mesh.shape["expert"], *args)

    step = jax.shard_map(
        step,
        mesh=mesh,
        in_specs=(
            P("dp", "expert", None, None, None),
            P(("dp", "expert"), None),
            P(("dp", "expert"), None),
        ),
        out_specs=(P(("dp", "expert"), None), P("expert"), P("expert")),
        check_vma=False,
    )
    return step
```

```python
import functools

import jax
import jax.numpy as jnp
from jax import lax
from jax.experimental import pallas as pl
from jax.experimental.pallas import tpu as pltpu
from jax.sharding import PartitionSpec as P


LANES = 128
GROUP = 8

epsilon = 1e-06

VMEM = pl.BlockSpec(memory_space=pltpu.VMEM)
SMEM = pl.BlockSpec(memory_space=pltpu.SMEM)
HBM = pl.BlockSpec(memory_space=pltpu.HBM)


def iota(shape, axis):
    return lax.broadcasted_iota(jnp.int32, shape, axis)


def params():
    return pltpu.CompilerParams(vmem_limit_bytes=16 << 20)


def near(x):
    return pltpu.with_memory_space_constraint(x, pltpu.VMEM)


def far(x):
    return pltpu.with_memory_space_constraint(x, pltpu.HBM)


def split(x):
    high = x.astype(jnp.bfloat16)
    return high, (x - high.astype(jnp.float32)).astype(jnp.bfloat16)


def weights_kernel(ids_hbm, gates_hbm, out_ref, ids_ref, gates_ref, sems):
    loads = [
        pltpu.make_async_copy(ids_hbm, ids_ref, sems.at[0]),
        pltpu.make_async_copy(gates_hbm, gates_ref, sems.at[1]),
    ]
    for copy in loads:
        copy.start()
    for copy in loads:
        copy.wait()
    tokens = out_ref.shape[0]
    ids, gates = ids_ref[...], gates_ref[...]
    shape = out_ref.shape
    lane, row = iota(shape, 1), iota(shape, 0)
    gate = jnp.zeros(shape, jnp.float32)
    named = jnp.zeros(shape, jnp.float32)
    for k in range(ids.shape[1]):
        same = jnp.broadcast_to(ids[:, k : k + 1], shape) == lane
        named = jnp.where(same, 1.0, named)
        gate = jnp.where(same, jnp.broadcast_to(gates[:, k : k + 1], shape), gate)
    upto, shift = named, 1
    while shift < tokens:
        upto = upto + jnp.where(row >= shift, pltpu.roll(upto, shift, 0), 0.0)
        shift *= 2
    out_ref[...] = jnp.where(upto - named > 0.5, -gate, gate)


def weights(ids, gates, experts):
    return pl.pallas_call(
        weights_kernel,
        out_shape=pltpu.VMEM((ids.shape[0], experts), jnp.float32),
        in_specs=[HBM, HBM],
        out_specs=VMEM,
        scratch_shapes=[
            pltpu.VMEM(ids.shape, ids.dtype),
            pltpu.VMEM(gates.shape, gates.dtype),
            pltpu.SemaphoreType.DMA((2,)),
        ],
        compiler_params=params(),
        name="weights",
    )(far(ids), far(gates))


def load_kernel(own_hbm, own_ref, sem):
    copy = pltpu.make_async_copy(own_hbm, own_ref, sem)
    copy.start()
    copy.wait()


def load(own):
    return pl.pallas_call(
        load_kernel,
        out_shape=pltpu.VMEM(own.shape, own.dtype),
        in_specs=[HBM],
        out_specs=VMEM,
        scratch_shapes=[pltpu.SemaphoreType.DMA],
        compiler_params=params(),
        name="load",
    )(far(own))


def squares_kernel(own_ref, out_ref):
    experts, holders, height, _ = own_ref.shape
    ones = jnp.ones((8, LANES), jnp.bfloat16)
    for e in range(experts):
        parts = []
        for s in range(holders):
            total = jnp.zeros((8, LANES), jnp.float32)
            for r in range(0, height, 16):
                part = own_ref[e, s, r : r + 16, :].astype(jnp.float32)
                total = total + part[:8] * part[:8] + part[8:] * part[8:]
            parts.append(total)
        total = jnp.concatenate(parts, axis=0)
        sums = jnp.zeros((8, holders * 8), jnp.float32)
        for term in split(total):
            sums = sums + lax.dot_general(
                ones, term, (((1,), (1,)), ((), ())), preferred_element_type=jnp.float32
            )
        out_ref[e] = sums


def squares(own):
    experts, holders, _, _ = own.shape
    return pl.pallas_call(
        squares_kernel,
        out_shape=pltpu.VMEM((experts, 8, holders * 8), jnp.float32),
        in_specs=[VMEM],
        out_specs=VMEM,
        compiler_params=params(),
        name="squares",
    )(near(own))


def statistics_kernel(mine_ref, theirs_ref, squares_ref, out_ref, *, cap):
    me = lax.axis_index("expert")
    chips, _, every = mine_ref.shape
    experts, _, wide = squares_ref.shape
    mine = jnp.where(
        iota((experts, every), 1) == me * experts + iota((experts, every), 0), 1.0, 0.0
    ).astype(jnp.bfloat16)
    slot = iota((experts, wide), 1) % cap
    row = iota((experts, wide), 0)
    total = jnp.zeros((experts, wide), jnp.float32)
    for core, ref in enumerate((mine_ref, theirs_ref)):
        signed = ref[...]
        source = (iota((chips, wide), 0) * 2 + core) ^ me
        spread = jnp.where(iota((chips, wide), 1) // 8 == source, 1.0, 0.0).astype(jnp.bfloat16)
        for c, used in enumerate((signed > 0.0, signed < 0.0)):
            used = jnp.max(jnp.where(used, 1.0, 0.0), axis=1).astype(jnp.bfloat16)
            used = lax.dot_general(
                mine, used, (((1,), (1,)), ((), ())), preferred_element_type=jnp.float32
            )
            used = jnp.dot(used.astype(jnp.bfloat16), spread, preferred_element_type=jnp.float32)
            total = total + jnp.where(slot == c, used, 0.0)
    square = jnp.zeros((experts, wide), jnp.float32)
    for e in range(experts):
        square = jnp.where(row == e, jnp.broadcast_to(squares_ref[e, 0:1, :], square.shape), square)
    ones = jnp.ones((8, wide), jnp.float32)
    sums, counts = [
        lax.dot_general(
            ones, x, (((1,), (1,)), ((), ())),
            precision=lax.Precision.HIGHEST, preferred_element_type=jnp.float32,
        )
        for x in (total * square, total * (cap / 8))
    ]
    out_ref[...] = jnp.where(iota(out_ref.shape, 0) == 0, sums, counts)


def statistics(mine, theirs, square, cap):
    return pl.pallas_call(
        functools.partial(statistics_kernel, cap=cap),
        out_shape=pltpu.VMEM((8, square.shape[0]), jnp.float32),
        in_specs=[VMEM, VMEM, VMEM],
        out_specs=VMEM,
        compiler_params=params(),
        name="statistics",
    )(near(mine), near(theirs), near(square))


def combine_kernel(signed_ref, own_ref, other_ref, *outs, sources, first, last, cap):
    me = lax.axis_index("expert")
    experts = own_ref.shape[0]
    tokens, every = signed_ref.shape[1:]
    rows = GROUP * cap
    depth = 2 * experts * rows
    lane = iota((every, depth), 1)
    holder = jnp.where(lane < experts * rows, me, me ^ 1)
    chosen = iota((every, depth), 0) == holder * experts + (lane // rows) % experts
    chosen = jnp.where(chosen, 1.0, 0.0).astype(jnp.bfloat16)
    signed = signed_ref[...].reshape(-1, every)
    high, low = split(signed)
    high = jnp.dot(high, chosen, preferred_element_type=jnp.float32)
    low = jnp.dot(low, chosen, preferred_element_type=jnp.float32)
    second = high < 0.0
    kept = second == (iota(high.shape, 1) % cap == 1)
    sign = jnp.where(second, -1.0, 1.0)
    high = jnp.where(kept, high * sign, 0.0)
    low = jnp.where(kept, low * sign, 0.0)
    tile = (iota((tokens, depth), 1) // cap) % GROUP
    half = GROUP * tokens
    for i, q in enumerate(sources):
        source = me ^ (2 * q)
        span = slice(i * tokens, (i + 1) * tokens)
        left = [jnp.where(tile == j, term[span], 0.0) for term in (high, low) for j in range(GROUP)]
        left = jnp.concatenate(left, axis=0).astype(jnp.bfloat16)
        for b in range(first, last):
            part = slice(b * rows, (b + 1) * rows)
            part = jnp.concatenate([own_ref[:, source, part, :], other_ref[:, source, part, :]], axis=0)
            total = jnp.dot(left, part.reshape(depth, LANES), preferred_element_type=jnp.float32)
            total = total[:half] + total[half:]
            outs[i][(b - first) * half : (b - first + 1) * half, :] = total.astype(outs[i].dtype)


def combine(signed, own, other, sources, first, last, cap, dtype):
    rows = (last - first) * GROUP
    return pl.pallas_call(
        functools.partial(combine_kernel, sources=sources, first=first, last=last, cap=cap),
        out_shape=[pltpu.VMEM((rows * signed.shape[1], LANES), dtype)] * len(sources),
        in_specs=[VMEM, VMEM, VMEM],
        out_specs=[VMEM] * len(sources),
        compiler_params=params(),
    )(near(signed), near(own), near(other))


def exchange(x, axis, size, bit):
    return lax.ppermute(x, axis, [(i, i ^ bit) for i in range(size)])


def body(dp, holders, expert_out, expert_ids, gate_weight):
    _, experts, _, cap, width = expert_out.shape
    tokens = expert_ids.shape[0]
    tiles = width // LANES
    groups = tiles // GROUP
    chips = holders // 2
    low = 1 << ((chips.bit_length() - 1) // 2)
    high = chips // low

    def swap(x, bit):
        return exchange(x, "expert", holders, bit)

    own = expert_out.reshape(experts, holders, cap, tiles, LANES)
    own = own.transpose(0, 1, 3, 2, 4).reshape(experts, holders, tiles * cap, LANES)
    other = swap(own, 1)
    tile = weights(expert_ids, gate_weight, experts * holders)
    signed = jnp.stack([tile] + [swap(tile, 2 * d) for d in range(1, low)])
    own = load(own)
    signed = [signed]
    for h in range(1, high):
        signed.append(swap(signed[0], 2 * low * h))

    def sums(pairs, first, last, dtype):
        tiles = jnp.concatenate([signed[h][d : d + 1] for h, d in pairs])
        sources = [h * low + d for h, d in pairs]
        return combine(tiles, own, other, sources, first, last, cap, dtype)

    part = sums([(1, d) for d in range(low)], 0, groups, jnp.bfloat16)
    near_sums = swap(jnp.stack(part), 2 * low).astype(jnp.float32)
    distant = list(range(2, high))
    half = (len(distant) + 1) // 2
    chunks = {"c": distant[:half], "d": distant[half:]}
    arrived = {}
    for key, hs in chunks.items():
        part = sums([(h, d) for d in range(1, low) for h in hs], 0, groups, jnp.bfloat16)
        part = jnp.stack(part).reshape(low - 1, len(hs), -1, LANES)
        arrived[key] = [swap(part[d - 1], 2 * d) for d in range(1, low)]
    kept = sums([(0, d) for d in range(low)] + [(h, 0) for h in distant], 0, groups, jnp.float32)
    combined = kept[0] + near_sums[0]
    for d in range(1, low):
        moved = swap((kept[d] + near_sums[d]).astype(jnp.bfloat16), 2 * d)
        combined = combined + moved.astype(jnp.float32)

    moved = []
    for key, hs in chunks.items():
        for i, h in enumerate(hs):
            out = kept[low + distant.index(h)]
            for m in arrived[key]:
                out = out + m[i].astype(jnp.float32)
            moved.append(swap(out.astype(jnp.bfloat16), 2 * low * h).astype(jnp.float32))

    for m in moved:
        combined = combined + m
    combined = combined.astype(jnp.bfloat16).reshape(tiles, tokens, LANES)
    combined = combined.transpose(1, 0, 2).reshape(tokens, width)

    signed = jnp.concatenate(signed)
    theirs = swap(signed, 1)
    square = squares(own)
    both = statistics(signed, theirs, square, cap)
    bit = 1
    while bit < dp:
        moved = exchange(both, "dp", dp, bit)
        both = both + moved
        bit *= 2
    squared, counts = both[0], both[1]
    expert_rms = jnp.sqrt(squared / (counts * width) + epsilon)
    counts = counts.astype(jnp.int32)
    return combined, counts, expert_rms


def solution(mesh):
    def step(*args):
        return body(mesh.shape["dp"], mesh.shape["expert"], *args)

    step = jax.shard_map(
        step,
        mesh=mesh,
        in_specs=(
            P("dp", "expert", None, None, None),
            P(("dp", "expert"), None),
            P(("dp", "expert"), None),
        ),
        out_specs=(P(("dp", "expert"), None), P("expert"), P("expert")),
        check_vma=False,
    )
    return step
```
